32 devices in a mesh: gene: 4 (over x, core), cell: 8 (over z, y).
Axes of the slice: x: 2, y: 2, z: 4, core: 2. Of those that a mesh axis runs over, the one named last changes fastest.
Arguments:
- data: bfloat16 [19968, 4096], P('gene', 'cell'), may hold values from 0.049804688 to 5
- labels: int32 [32, 1], P('cell'), may hold values from 0 to 1; in each aligned block of 4 rows (0 to 3, 4 to 7, ...) at most 3 rows name the same one
- w_init: float32 [2, 19968], P(None, 'gene'), may hold values from 0.1 to 1
- h_init: float32 [2, 4096], P(None, 'cell'), may hold values from 0.1 to 2
Outputs:
- w_factor: float32 [2, 19968], P(None, 'gene')
- h_factor: float32 [2, 4096], P(None, 'cell')
- children: bfloat16 [19968, 8192], P('gene', 'cell')
The draws below stay inside these ranges and needn't reach their ends.
Inputs may be any that keep to these rules, and one draw needn't show every extreme that they name: labels are 0 or 1; among the 4 blocks of one group of cells no label occurs more than 3 times, and some group reaches 3.
All inputs are finite; a program needn't handle non-finite values.
Results may differ from the reference program's by a relative error of at most 0.00057.
Values may be sent and summed in bfloat16 or wider, within the bound.
No kernel may reach another device: no remote copies, remote signals or barrier semaphores. Data moves between devices by JAX's collectives and lax.ppermute only.
A program may use at most 64 MiB of HBM per device.

```python
import math
import jax
import jax.numpy as jnp
import numpy as np
from jax import lax

G = 19968
RANK = 2
ITERS = 2
BLOCK = 128
BLK_DEV = 4
MOST = 3
CELLS = 4096
NBLK = 32
N_CELL = 8


def steps_of(rng, shape, cuts, least, top_value):
    gain, own = 1.0, jax.random.fold_in(rng, 6)
    for axis_at, parts in cuts:
        draws = jnp.exp(jax.random.uniform(jax.random.fold_in(own, axis_at), (parts,), jnp.float32, least / len(cuts), top_value / len(cuts)))
        gain = gain * jnp.repeat(draws, shape[axis_at] // parts).reshape([-1 if axis == axis_at else 1 for axis in range(len(shape))])
    return gain


def shared_out(stream_key, own, number, rows, amount, top, bound, slope):
    ranking = jax.random.permutation(stream_key, amount)
    packed, usual = load_shares(amount, rows * top, bound, slope, True), load_shares(amount, rows * top, bound, slope, False)
    places = jnp.arange(amount)

    def named(lengths, turn):
        used = int((lengths > 0).sum())
        fixed = max(1, used // 4)
        moved = fixed + (places - fixed + turn * (used - fixed)) % max(1, amount - fixed)
        return jnp.zeros((amount,), jnp.int32).at[ranking[jnp.where(places < fixed, places, moved)]].set(jnp.asarray(lengths, jnp.int32))

    lengths = jnp.where(number % 4 == 0, named(packed, number // 4), named(usual, number - number // 4 - 1))
    mixed = jax.random.permutation(jax.random.fold_in(own, 3), amount)
    giver, sink = mixed[0:amount // 2 * 2:2], mixed[1:amount // 2 * 2:2]
    room = jnp.minimum(lengths[giver] - 1, bound - lengths[sink]) // 2
    room = jnp.where((giver == ranking[0]) | (sink == ranking[0]) | (lengths[sink] == 0), 0, jnp.maximum(room, 0))
    moved = jax.random.randint(jax.random.fold_in(own, 4), (amount // 2,), 0, 1 << 20) % (room + 1)
    lengths = lengths.at[giver].add(-moved).at[sink].add(moved)
    items = jnp.searchsorted(jnp.cumsum(lengths), jnp.arange(rows * top), side="right").astype(jnp.int32)
    grid = items.reshape(top, rows).T
    grid = grid[jax.random.permutation(jax.random.fold_in(own, 1), rows)]
    turn = jax.random.randint(jax.random.fold_in(own, 2), (rows, 1), 0, top)
    return jnp.take_along_axis(grid, (jnp.arange(top)[None, :] + turn) % top, axis=1)


def load_shares(count, total, bound, slope, full):
    weights = [(1 << 20) // math.isqrt(grade ** slope) + 1 for grade in range(1, count + 1)]
    largest = bound if full else min(bound, max(-(-total // count), total * weights[0] // sum(weights)))
    least = 1 if total - largest >= count - 1 else 0
    given, surplus = [largest] + [least] * (count - 1), total - largest - least * (count - 1)
    while surplus > 0:
        candidates = [i for i in range(1, count) if given[i] < largest] or [i for i in range(1, count) if given[i] < bound]
        whole, budget = sum([weights[i] for i in candidates]), surplus
        for i in candidates:
            extra = min(bound - given[i], max(1, budget * weights[i] // whole), surplus)
            given[i] = given[i] + extra
            surplus = surplus - extra
    return np.array(given)


def setup_inputs(seed: int = 0) -> dict:
    key_list = jax.random.split(jax.random.key(seed), 5)
    data = jnp.clip(jnp.exp(math.log(5.0) - 4.609084 * jax.random.uniform(key_list[0], (G, CELLS), jnp.float32) ** steps_of(key_list[0], (G, CELLS), ((0, 4), (1, 8)), -0.2, 0.2)), 0.049804688, 5.0).astype(jnp.bfloat16)
    labels_keys = jax.random.split(jax.random.fold_in(key_list[1], 1), NBLK // BLK_DEV)
    labels_turns = jax.random.permutation(jax.random.fold_in(key_list[1], 3), NBLK // BLK_DEV)
    labels = jax.vmap(lambda own, number: shared_out(jax.random.fold_in(key_list[1], 2), own, number, BLK_DEV, 2, 1, MOST, 0))(labels_keys, labels_turns).reshape((NBLK, 1))
    w_init = jnp.clip(jnp.exp(math.log(1.0) - 2.3025851 * jax.random.uniform(key_list[2], (RANK, G), jnp.float32) ** steps_of(key_list[2], (RANK, G), ((1, 4),), -0.2, 0.2)), 0.1, 1.0)
    h_init = jnp.clip(jnp.exp(math.log(2.0) - 2.9957323 * jax.random.uniform(key_list[3], (RANK, CELLS), jnp.float32) ** steps_of(key_list[3], (RANK, CELLS), ((1, 8),), -0.2, 0.2)), 0.1, 2.0)
    return dict(data=data, labels=labels, w_init=w_init, h_init=h_init)


FLOOR = 1e-4
GRAM_EPS = 1e-6


def update_rows(factor, numer, gram):
    first = jnp.maximum(factor[0] + (numer[0] - gram[0, 0] * factor[0] - gram[0, 1] * factor[1]) / (gram[0, 0] + GRAM_EPS), FLOOR)
    second = jnp.maximum(factor[1] + (numer[1] - gram[1, 0] * first - gram[1, 1] * factor[1]) / (gram[1, 1] + GRAM_EPS), FLOOR)
    return jnp.stack([first, second])


def reference(data, labels, w_init, h_init):
    w_factor = w_init
    h_factor = h_init
    for step in range(ITERS):
        w_round = w_factor.astype(jnp.bfloat16)
        w_data = jnp.dot(w_round, data, preferred_element_type=jnp.float32)
        w_gram = jnp.dot(w_round, w_round.T, preferred_element_type=jnp.float32)
        h_factor = update_rows(h_factor, w_data, w_gram)
        h_round = h_factor.astype(jnp.bfloat16)
        h_data = lax.dot_general(h_round, data, (((1,), (1,)), ((), ())), preferred_element_type=jnp.float32)
        h_gram = jnp.dot(h_round, h_round.T, preferred_element_type=jnp.float32)
        w_factor = update_rows(w_factor, h_data, h_gram)
    groups = N_CELL
    width = CELLS // groups
    col_label = jnp.repeat(labels[:, 0], BLOCK).reshape(groups, width)
    half = (jnp.arange(groups) >= groups // 2).astype(jnp.int32)
    shaped = data.reshape(G, groups, width)
    zero = jnp.zeros((), jnp.bfloat16)
    own = jnp.where((col_label == half[:, None])[None], shaped, zero)
    partner_label = jnp.roll(col_label, groups // 2, axis=0)
    partner_data = jnp.roll(shaped, groups // 2, axis=1)
    other = jnp.where((partner_label == half[:, None])[None], partner_data, zero)
    children = jnp.concatenate([own, other], axis=2).reshape(G, 2 * CELLS)
    return w_factor, h_factor, children
```

```python
import functools

import jax
import jax.numpy as jnp
from jax import lax
from jax.experimental import pallas as pl
from jax.experimental.pallas import tpu as pltpu
from jax.sharding import PartitionSpec as P

ITERS = 2
BLOCK = 128

FLOOR = 0.0001
GRAM_EPS = 1e-06


def flipped(x, axis, mask):
    count = lax.axis_size(axis)
    return lax.ppermute(x, axis, [(i, i ^ mask) for i in range(count)])


def all_sum(x, axis):
    count = lax.axis_size(axis)
    if count & (count - 1):
        return lax.psum(x, axis)
    bit = count
    while bit > 1:
        high, low = bit >> 1, bit >> 2
        if low:
            x = (x + flipped(x, axis, low)) + (flipped(x, axis, high) + flipped(x, axis, high | low))
        else:
            x = x + flipped(x, axis, high)
        bit = low or high
        if not low:
            break
    return x


def update_rows(factor, numer, gram):
    first = jnp.maximum(
        factor[0]
        + (numer[0] - gram[0, 0] * factor[0] - gram[0, 1] * factor[1]) / (gram[0, 0] + GRAM_EPS),
        FLOOR,
    )
    second = jnp.maximum(
        factor[1]
        + (numer[1] - gram[1, 0] * first - gram[1, 1] * factor[1]) / (gram[1, 1] + GRAM_EPS),
        FLOOR,
    )
    return jnp.stack([first, second])


def nth(flags, blocks, turn):
    leaving = sum(1 - flags[b] for b in range(blocks))
    found, low, high = 0, 0, leaving
    for b in range(blocks):
        rank = jnp.where(flags[b] > 0, high, low)
        found = found + jnp.where(rank == turn, b, 0)
        low, high = low + 1 - flags[b], high + flags[b]
    return found


def pack_kernel(flags, data, after, out):
    out[0] = data[...]


def pack(flags, data, after, first, count, parts):
    rows = data.shape[0] // parts
    blocks = data.shape[1] // BLOCK
    return pl.pallas_call(
        pack_kernel,
        grid_spec=pltpu.PrefetchScalarGridSpec(
            num_scalar_prefetch=1,
            grid=(count,),
            in_specs=[
                pl.BlockSpec(
                    (rows, BLOCK), lambda i, f: ((first + i) % parts, nth(f, blocks, (first + i) // parts))
                ),
                pl.BlockSpec(memory_space=pl.ANY),
            ],
            out_specs=pl.BlockSpec((1, rows, BLOCK), lambda i, f: (i, 0, 0)),
        ),
        out_shape=jax.ShapeDtypeStruct((count, rows, BLOCK), data.dtype),
        cost_estimate=pl.CostEstimate(flops=0, bytes_accessed=4 * count * rows * BLOCK, transcendentals=0),
    )(flags, data, after)


def keep_kernel(blocks, flags, data, after, out):
    for b in range(blocks):
        cols = slice(b * BLOCK, (b + 1) * BLOCK)
        kept = flags[b] > 0
        out[:, cols] = jnp.where(kept, data[:, cols], jnp.zeros_like(data[:, cols]))
    out[:, blocks * BLOCK :] = jnp.zeros((out.shape[0], blocks * BLOCK), out.dtype)


def keep(flags, data, after):
    rows, cols = data.shape
    tile = next(t for t in (624, 312, 208, 16, rows) if rows % t == 0)
    return pl.pallas_call(
        functools.partial(keep_kernel, cols // BLOCK),
        grid_spec=pltpu.PrefetchScalarGridSpec(
            num_scalar_prefetch=1,
            grid=(rows // tile,),
            in_specs=[
                pl.BlockSpec((tile, cols), lambda i, f: (i, 0)),
                pl.BlockSpec(memory_space=pl.ANY),
            ],
            out_specs=pl.BlockSpec((tile, 2 * cols), lambda i, f: (i, 0)),
        ),
        out_shape=jax.ShapeDtypeStruct((rows, 2 * cols), data.dtype),
        cost_estimate=pl.CostEstimate(flops=0, bytes_accessed=6 * rows * cols, transcendentals=0),
        name="keep",
    )(flags, data, after)


def place_kernel(first, parts, blocks, flags, got, held, out):
    sent = sum(1 - flags[b] for b in range(blocks))
    valid = (first + pl.program_id(0)) // parts < sent
    out[...] = jnp.where(valid, got[0], jnp.zeros_like(got[0]))


def place(flags, got, held, first, parts):
    _, cols = held.shape
    blocks = cols // BLOCK // 2
    count, tile, _ = got.shape
    return pl.pallas_call(
        functools.partial(place_kernel, first, parts, blocks),
        grid_spec=pltpu.PrefetchScalarGridSpec(
            num_scalar_prefetch=1,
            grid=(count,),
            in_specs=[
                pl.BlockSpec((1, tile, BLOCK), lambda i, f: (i, 0, 0)),
                pl.BlockSpec(memory_space=pl.ANY),
            ],
            out_specs=pl.BlockSpec(
                (tile, BLOCK),
                lambda i, f: ((first + i) % parts, blocks + nth(f, blocks, (first + i) // parts)),
            ),
        ),
        out_shape=jax.ShapeDtypeStruct(held.shape, held.dtype),
        input_output_aliases={2: 0},
        cost_estimate=pl.CostEstimate(flops=0, bytes_accessed=4 * count * tile * BLOCK, transcendentals=0),
    )(flags, got, held)


def with_gram(part, factor):
    gram = jnp.dot(factor, factor.T, preferred_element_type=jnp.float32)
    return jnp.concatenate([part, jnp.pad(gram, ((0, 0), (0, BLOCK - factor.shape[0])))], axis=1)


def steps(data, labels, w_init, h_init):
    rows, cols = data.shape
    blocks = cols // BLOCK
    groups = lax.axis_size("cell")
    across = groups // 2
    half = (lax.axis_index("cell") >= across).astype(jnp.int32)
    most = blocks - max(1, blocks // 4)
    parts = next(p for p in (4, 2, 1) if rows % (16 * p) == 0)
    flags = (labels[:, 0] == half).astype(jnp.int32)
    always = max(1, most - 1) * parts
    cuts = [0, always // 4, always * 5 // 8, always]
    packed = [
        pack(flags, data, w_init, cuts[i], cuts[i + 1] - cuts[i], parts) for i in range(len(cuts) - 1)
    ]

    def send(i):
        return flipped(packed[i], "cell", across)

    got = [send(0)]
    flags_in = flipped(flags, "cell", across)
    w_factor = w_init
    h_factor = h_init
    for step in range(ITERS):
        w_round = w_factor.astype(jnp.bfloat16)
        w_part = jnp.dot(w_round, data, preferred_element_type=jnp.float32)
        w_sum = all_sum(with_gram(w_part, w_round), "gene")
        h_factor = update_rows(h_factor, w_sum[:, :cols], w_sum[:, cols : cols + 2])
        h_round = h_factor.astype(jnp.bfloat16)
        h_part = lax.dot_general(
            h_round, data, (((1,), (1,)), ((), ())), preferred_element_type=jnp.float32
        )
        h_sum = all_sum(with_gram(h_part, h_round), "cell")
        if step + 1 < len(cuts) - 1:
            got.append(send(step + 1))
        w_factor = update_rows(w_factor, h_sum[:, :rows], h_sum[:, rows : rows + 2])
    last = pack(flags, data, w_factor, always, most * parts - always, parts)
    needed = (blocks - jnp.minimum(jnp.sum(flags), jnp.sum(flags_in))) * parts > always
    late = lax.cond(needed, lambda x: flipped(x, "cell", across), lambda x: x, last)
    children = keep(flags, data, w_factor)
    for i, x in enumerate(got):
        children = place(flags_in, x, children, cuts[i], parts)
    children = place(flags_in, late, children, always, parts)
    return (w_factor, h_factor, children)


def solution(mesh):
    placed = (P("gene", "cell"), P("cell", None), P(None, "gene"), P(None, "cell"))
    return jax.shard_map(
        steps,
        mesh=mesh,
        in_specs=placed,
        out_specs=(P(None, "gene"), P(None, "cell"), P("gene", "cell")),
        check_vma=False,
    )
```

```python
import functools

import jax
import jax.numpy as jnp
from jax import lax
from jax.experimental import pallas as pl
from jax.experimental.pallas import tpu as pltpu
from jax.sharding import PartitionSpec as P

ITERS = 2
BLOCK = 128

FLOOR = 0.0001
GRAM_EPS = 1e-06


def flipped(x, axis, mask):
    count = lax.axis_size(axis)
    return lax.ppermute(x, axis, [(i, i ^ mask) for i in range(count)])


def all_sum(x, axis):
    count = lax.axis_size(axis)
    if count & (count - 1):
        return lax.psum(x, axis)
    bit = count
    while bit > 1:
        high, low = bit >> 1, bit >> 2
        if low:
            x = (x + flipped(x, axis, low)) + (flipped(x, axis, high) + flipped(x, axis, high | low))
        else:
            x = x + flipped(x, axis, high)
        bit = low or high
        if not low:
            break
    return x


def update_rows(factor, numer, gram):
    first = jnp.maximum(
        factor[0]
        + (numer[0] - gram[0, 0] * factor[0] - gram[0, 1] * factor[1]) / (gram[0, 0] + GRAM_EPS),
        FLOOR,
    )
    second = jnp.maximum(
        factor[1]
        + (numer[1] - gram[1, 0] * first - gram[1, 1] * factor[1]) / (gram[1, 1] + GRAM_EPS),
        FLOOR,
    )
    return jnp.stack([first, second])


def runs(first, count, parts):
    found, at = [], first
    while at < first + count:
        size = min(parts - at % parts, first + count - at)
        found.append((at // parts, at % parts, size, at - first))
        at += size
    return found


def nth(leaves, turn):
    found, low, high = 0, 0, sum(leaves)
    for b, leave in enumerate(leaves):
        found = found + jnp.where(jnp.where(leave > 0, low, high) == turn, b, 0)
        low, high = low + leave, high + 1 - leave
    return found


def my_half():
    return (lax.axis_index("cell") >= lax.axis_size("cell") // 2).astype(jnp.int32)


def lanes(block):
    return pl.ds(pl.multiple_of(block * BLOCK, BLOCK), BLOCK)


def pack_kernel(first, parts, labels, data, out, sems):
    tile = data.shape[0] // parts
    half = my_half()
    leaves = [(labels[b] != half).astype(jnp.int32) for b in range(data.shape[1] // BLOCK)]
    copies = []
    for n, (block, at, size, before) in enumerate(runs(first, out.shape[0] // tile, parts)):
        copies.append(
            pltpu.make_async_copy(
                data.at[pl.ds(at * tile, size * tile), lanes(nth(leaves, block))],
                out.at[pl.ds(before * tile, size * tile), :],
                sems.at[n],
            )
        )
        copies[-1].start()
    for copy in copies:
        copy.wait()


def pack(labels, data, first, count, parts):
    shape = (count * data.shape[0] // parts, BLOCK)
    return pl.pallas_call(
        functools.partial(pack_kernel, first, parts),
        in_specs=[pl.BlockSpec(memory_space=pltpu.SMEM), pl.BlockSpec(memory_space=pl.ANY)],
        out_specs=pl.BlockSpec(memory_space=pltpu.VMEM),
        out_shape=jax.ShapeDtypeStruct(shape, data.dtype),
        scratch_shapes=[pltpu.SemaphoreType.DMA((len(runs(first, count, parts)),))],
        cost_estimate=pl.CostEstimate(flops=0, bytes_accessed=4 * shape[0] * BLOCK, transcendentals=0),
    )(labels, data)


def keep_kernel(blocks, labels, data, out):
    half = my_half()
    for b in range(blocks):
        cols = slice(b * BLOCK, (b + 1) * BLOCK)
        out[:, cols] = jnp.where(labels[b] == half, data[:, cols], jnp.zeros_like(data[:, cols]))
    out[:, blocks * BLOCK :] = jnp.zeros((out.shape[0], blocks * BLOCK), out.dtype)


def keep(labels, data):
    rows, cols = data.shape
    tile = next(t for t in (624, 312, 208, 16, rows) if rows % t == 0)
    return pl.pallas_call(
        functools.partial(keep_kernel, cols // BLOCK),
        grid=(rows // tile,),
        in_specs=[pl.BlockSpec(memory_space=pltpu.SMEM), pl.BlockSpec((tile, cols), lambda i: (i, 0))],
        out_specs=pl.BlockSpec((tile, 2 * cols), lambda i: (i, 0)),
        out_shape=jax.ShapeDtypeStruct((rows, 2 * cols), data.dtype),
        cost_estimate=pl.CostEstimate(flops=0, bytes_accessed=6 * rows * cols, transcendentals=0),
        name="keep",
    )(labels, data)


def place_kernel(pieces, parts, labels, *refs):
    got, out, sems = refs[: len(pieces)], refs[-2], refs[-1]
    tile = out.shape[0] // parts
    blocks = out.shape[1] // BLOCK // 2
    half = my_half()
    leaves = [(labels[b] == half).astype(jnp.int32) for b in range(blocks)]
    copies = []
    for ref, first in zip(got, pieces):
        for block, at, size, before in runs(first, ref.shape[0] // tile, parts):
            copy = pltpu.make_async_copy(
                ref.at[pl.ds(before * tile, size * tile), :],
                out.at[pl.ds(at * tile, size * tile), lanes(blocks + nth(leaves, block))],
                sems.at[len(copies)],
            )
            copies.append((block < sum(leaves), copy))
    for valid, copy in copies:
        pl.when(valid)(copy.start)
    for valid, copy in copies:
        pl.when(valid)(copy.wait)


def place(labels, got, held, pieces, parts):
    tile = held.shape[0] // parts
    count = sum(len(runs(first, x.shape[0] // tile, parts)) for x, first in zip(got, pieces))
    moved = sum(x.size for x in got)
    return pl.pallas_call(
        functools.partial(place_kernel, pieces, parts),
        in_specs=[pl.BlockSpec(memory_space=pltpu.SMEM)]
        + [pl.BlockSpec(memory_space=pltpu.VMEM)] * len(got)
        + [pl.BlockSpec(memory_space=pl.ANY)],
        out_specs=pl.BlockSpec(memory_space=pl.ANY),
        out_shape=jax.ShapeDtypeStruct(held.shape, held.dtype),
        input_output_aliases={len(got) + 1: 0},
        scratch_shapes=[pltpu.SemaphoreType.DMA((count,))],
        cost_estimate=pl.CostEstimate(flops=0, bytes_accessed=4 * moved, transcendentals=0),
    )(labels, *got, held)


def with_gram(part, factor):
    gram = jnp.dot(factor, factor.T, preferred_element_type=jnp.float32)
    return jnp.concatenate([part, jnp.pad(gram, ((0, 0), (0, BLOCK - factor.shape[0])))], axis=1)


def steps(data, labels, w_init, h_init):
    rows, cols = data.shape
    blocks = cols // BLOCK
    groups = lax.axis_size("cell")
    across = groups // 2
    odd = lax.axis_index("cell") & 1
    most = blocks - max(1, blocks // 4)
    parts = next(p for p in (8, 4, 2) if rows % (16 * p) == 0)
    labels = labels[:, 0]
    always = max(1, most - 1) * parts
    rest = most * parts - always
    cuts = [always * share // 16 for share in SHARES]
    packed = [pack(labels, data, cuts[i], cuts[i + 1] - cuts[i], parts) for i in range(len(cuts) - 1)]
    own_0 = pack(labels, data, always, rest // 2, parts)
    own_1 = pack(labels, data, always + rest // 2, rest - rest // 2, parts)

    def send(i):
        return flipped(packed[i], "cell", across)

    got = [send(0)]
    lent = flipped(own_1, "cell", 1)
    labels_in = flipped(labels, "cell", across)
    half = my_half()
    leaving = jnp.maximum(jnp.sum((labels != half).astype(jnp.int32)), jnp.sum((labels_in == half).astype(jnp.int32)))
    need = (leaving * parts > always).astype(jnp.int32)
    need_beside = flipped(need[None], "cell", 1)[0]
    w_factor = w_init
    h_factor = h_init
    children = keep(labels, data)
    for step in range(ITERS):
        w_round = w_factor.astype(jnp.bfloat16)
        w_part = jnp.dot(w_round, data, preferred_element_type=jnp.float32)
        w_sum = all_sum(with_gram(w_part, w_round), "gene")
        h_factor = update_rows(h_factor, w_sum[:, :cols], w_sum[:, cols : cols + 2])
        h_round = h_factor.astype(jnp.bfloat16)
        h_part = lax.dot_general(
            h_round, data, (((1,), (1,)), ((), ())), preferred_element_type=jnp.float32
        )
        h_sum = all_sum(with_gram(h_part, h_round), "cell")
        got.append(send(step + 1))
        w_factor = update_rows(w_factor, h_sum[:, :rows], h_sum[:, rows : rows + 2])
    for i in range(len(got) - 1):
        children = place(labels_in, [got[i]], children, [cuts[i]], parts)

    def late(parity):
        def exchange(own, beside):
            return (
                lax.ppermute(own, "cell", [(i, i ^ across) for i in range(groups) if i % 2 == parity]),
                lax.ppermute(beside, "cell", [(i ^ 1, i ^ across) for i in range(groups) if i % 2 == parity]),
            )

        return exchange

    def late_both(own, beside):
        return flipped(own, "cell", across), flipped(beside, "cell", across | 1)

    wanted = (need << odd) + (need_beside << (1 - odd))
    last = lax.switch(wanted, [lambda *x: x, late(0), late(1), late_both], own_0, lent)
    children = place(
        labels_in, [got[-1], *last], children, [cuts[-2], always, always + rest // 2], parts
    )
    return (w_factor, h_factor, children)


SHARES = (0, 5, 12, 16)


def solution(mesh):
    placed = (P("gene", "cell"), P("cell", None), P(None, "gene"), P(None, "cell"))
    return jax.shard_map(
        steps,
        mesh=mesh,
        in_specs=placed,
        out_specs=(P(None, "gene"), P(None, "cell"), P("gene", "cell")),
        check_vma=False,
    )
```

```python
import functools

import jax
import jax.numpy as jnp
from jax import lax
from jax.experimental import pallas as pl
from jax.experimental.pallas import tpu as pltpu
from jax.sharding import PartitionSpec as P

ITERS = 2
BLOCK = 128

FLOOR = 0.0001
GRAM_EPS = 1e-06


def flipped(x, axis, mask):
    count = lax.axis_size(axis)
    return lax.ppermute(x, axis, [(i, i ^ mask) for i in range(count)])


def all_sum(x, axis, bit):
    while bit > 1:
        high, low = bit >> 1, bit >> 2
        if low:
            x = (x + flipped(x, axis, low)) + (flipped(x, axis, high) + flipped(x, axis, high | low))
        else:
            x = x + flipped(x, axis, high)
        bit = low
    return x


def row_sum(x, axis):
    odd = lax.axis_index(axis) & 1
    mine = jnp.where(odd > 0, x[1:], x[:1]) + flipped(jnp.where(odd > 0, x[:1], x[1:]), axis, 1)
    count, bit = lax.axis_size(axis), 2
    while bit < count:
        both = bit << 1 < count
        if both:
            high = bit << 1
            mine = (mine + flipped(mine, axis, bit)) + (flipped(mine, axis, high) + flipped(mine, axis, high | bit))
        else:
            mine = mine + flipped(mine, axis, bit)
        bit = bit << (2 if both else 1)
    return mine


def join_rows(mine, axis):
    odd = lax.axis_index(axis) & 1
    other = flipped(mine, axis, 1)
    return jnp.concatenate([jnp.where(odd > 0, other, mine), jnp.where(odd > 0, mine, other)])


def update_rows(factor, numer, gram):
    first = jnp.maximum(
        factor[0]
        + (numer[0] - gram[0, 0] * factor[0] - gram[0, 1] * factor[1]) / (gram[0, 0] + GRAM_EPS),
        FLOOR,
    )
    second = jnp.maximum(
        factor[1]
        + (numer[1] - gram[1, 0] * first - gram[1, 1] * factor[1]) / (gram[1, 1] + GRAM_EPS),
        FLOOR,
    )
    return jnp.stack([first, second])


def runs(first, count, parts):
    found, at = [], first
    while at < first + count:
        size = min(parts - at % parts, first + count - at)
        found.append((at // parts, at % parts, size, at - first))
        at += size
    return found


def nth(leaves, turn):
    found, low, high = 0, 0, sum(leaves)
    for b, leave in enumerate(leaves):
        found = found + jnp.where(jnp.where(leave > 0, low, high) == turn, b, 0)
        low, high = low + leave, high + 1 - leave
    return found


def my_half():
    return (lax.axis_index("cell") >= lax.axis_size("cell") // 2).astype(jnp.int32)


def lanes(block):
    return pl.ds(pl.multiple_of(block * BLOCK, BLOCK), BLOCK)


def pack_kernel(first, parts, labels, data, out, sems):
    tile = data.shape[0] // parts
    half = my_half()
    leaves = [(labels[b] != half).astype(jnp.int32) for b in range(data.shape[1] // BLOCK)]
    copies = []
    for n, (block, at, size, before) in enumerate(runs(first, out.shape[0] // tile, parts)):
        copies.append(
            pltpu.make_async_copy(
                data.at[pl.ds(at * tile, size * tile), lanes(nth(leaves, block))],
                out.at[pl.ds(before * tile, size * tile), :],
                sems.at[n],
            )
        )
        copies[-1].start()
    for copy in copies:
        copy.wait()


def pack(labels, data, first, count, parts):
    shape = (count * data.shape[0] // parts, BLOCK)
    return pl.pallas_call(
        functools.partial(pack_kernel, first, parts),
        in_specs=[pl.BlockSpec(memory_space=pltpu.SMEM), pl.BlockSpec(memory_space=pl.ANY)],
        out_specs=pl.BlockSpec(memory_space=pltpu.VMEM),
        out_shape=pltpu.VMEM(shape, data.dtype),
        scratch_shapes=[pltpu.SemaphoreType.DMA((len(runs(first, count, parts)),))],
        cost_estimate=pl.CostEstimate(flops=0, bytes_accessed=4 * shape[0] * BLOCK, transcendentals=0),
    )(labels, data)


def keep_kernel(blocks, labels, data, out):
    half = my_half()
    for b in range(blocks):
        cols = slice(b * BLOCK, (b + 1) * BLOCK)
        out[:, cols] = jnp.where(labels[b] == half, data[:, cols], jnp.zeros_like(data[:, cols]))
    out[:, blocks * BLOCK :] = jnp.zeros((out.shape[0], blocks * BLOCK), out.dtype)


def keep(labels, data):
    rows, cols = data.shape
    tile = next(t for t in (624, 312, 208, 16, rows) if rows % t == 0)
    return pl.pallas_call(
        functools.partial(keep_kernel, cols // BLOCK),
        grid=(rows // tile,),
        in_specs=[pl.BlockSpec(memory_space=pltpu.SMEM), pl.BlockSpec((tile, cols), lambda i: (i, 0))],
        out_specs=pl.BlockSpec((tile, 2 * cols), lambda i: (i, 0)),
        out_shape=jax.ShapeDtypeStruct((rows, 2 * cols), data.dtype),
        cost_estimate=pl.CostEstimate(flops=0, bytes_accessed=6 * rows * cols, transcendentals=0),
        name="keep",
    )(labels, data)


def place_kernel(pieces, parts, labels, *refs):
    got, out, sems = refs[: len(pieces)], refs[-2], refs[-1]
    tile = out.shape[0] // parts
    blocks = out.shape[1] // BLOCK // 2
    half = my_half()
    leaves = [(labels[b] == half).astype(jnp.int32) for b in range(blocks)]
    copies = []
    for ref, first in zip(got, pieces):
        for block, at, size, before in runs(first, ref.shape[0] // tile, parts):
            copy = pltpu.make_async_copy(
                ref.at[pl.ds(before * tile, size * tile), :],
                out.at[pl.ds(at * tile, size * tile), lanes(blocks + nth(leaves, block))],
                sems.at[len(copies)],
            )
            copies.append((block < sum(leaves), copy))
    for valid, copy in copies:
        pl.when(valid)(copy.start)
    for valid, copy in copies:
        pl.when(valid)(copy.wait)


def place(labels, got, held, pieces, parts):
    tile = held.shape[0] // parts
    count = sum(len(runs(first, x.shape[0] // tile, parts)) for x, first in zip(got, pieces))
    moved = sum(x.size for x in got)
    return pl.pallas_call(
        functools.partial(place_kernel, pieces, parts),
        in_specs=[pl.BlockSpec(memory_space=pltpu.SMEM)]
        + [pl.BlockSpec(memory_space=pltpu.VMEM)] * len(got)
        + [pl.BlockSpec(memory_space=pl.ANY)],
        out_specs=pl.BlockSpec(memory_space=pl.ANY),
        out_shape=jax.ShapeDtypeStruct(held.shape, held.dtype),
        input_output_aliases={len(got) + 1: 0},
        scratch_shapes=[pltpu.SemaphoreType.DMA((count,))],
        cost_estimate=pl.CostEstimate(flops=0, bytes_accessed=4 * moved, transcendentals=0),
    )(labels, *got, held)


def with_gram(part, factor):
    gram = jnp.dot(factor, factor.T, preferred_element_type=jnp.float32)
    return jnp.concatenate([part, jnp.pad(gram, ((0, 0), (0, BLOCK - factor.shape[0])))], axis=1)


def steps(data, labels, w_init, h_init):
    rows, cols = data.shape
    blocks = cols // BLOCK
    groups = lax.axis_size("cell")
    across = groups // 2
    odd = lax.axis_index("cell") & 1
    most = blocks - max(1, blocks // 4)
    parts = next(p for p in (8, 4, 2) if rows % (16 * p) == 0)
    labels = labels[:, 0]
    always = max(1, most - 1) * parts
    rest = most * parts - always
    cuts = [always * share // 16 for share in SHARES]
    packed = []
    for i in range(len(cuts) - 1):
        packed.append(pack(labels, data, cuts[i], cuts[i + 1] - cuts[i], parts))
    own_0 = pack(labels, data, always, rest // 2, parts)
    own_1 = pack(labels, data, always + rest // 2, rest - rest // 2, parts)

    def send(i):
        return flipped(packed[i], "cell", across)

    got = [send(0)]
    lent = flipped(own_1, "cell", 1)
    labels_in = flipped(labels, "cell", across)
    half = my_half()
    leaving = jnp.maximum(jnp.sum((labels != half).astype(jnp.int32)), jnp.sum((labels_in == half).astype(jnp.int32)))
    need = (leaving * parts > always).astype(jnp.int32)
    need_beside = flipped(need[None], "cell", 1)[0]
    w_factor = w_init
    h_factor = h_init
    children = keep(labels, data)
    for step in range(ITERS):
        w_round = w_factor.astype(jnp.bfloat16)
        w_part = jnp.dot(w_round, data, preferred_element_type=jnp.float32)
        w_sum = all_sum(with_gram(w_part, w_round), "gene", lax.axis_size("gene"))
        h_factor = update_rows(h_factor, w_sum[:, :cols], w_sum[:, cols : cols + 2])
        h_round = h_factor.astype(jnp.bfloat16)
        h_part = lax.dot_general(
            h_round, data, (((1,), (1,)), ((), ())), preferred_element_type=jnp.float32
        )
        h_row = row_sum(with_gram(h_part, h_round), "cell")
        got.append(send(step + 1))

        def finish(w_factor, h_row):
            h_sum = join_rows(h_row, "cell")
            return update_rows(w_factor, h_sum[:, :rows], h_sum[:, rows : rows + 2])

        if step + 1 < ITERS:
            w_factor = finish(w_factor, h_row)
    children = place(labels_in, got[:-1], children, cuts[:-2], parts)

    def late_none(own, beside, w_factor, h_row):
        return jnp.zeros_like(own), jnp.zeros_like(beside), finish(w_factor, h_row)

    def late_one(parity):
        def exchange(own, beside, w_factor, h_row):
            return (
                lax.ppermute(own, "cell", [(i, i ^ across) for i in range(groups) if i % 2 == parity]),
                lax.ppermute(beside, "cell", [(i ^ 1, i ^ across) for i in range(groups) if i % 2 == parity]),
                finish(w_factor, h_row),
            )

        return exchange

    def late_both(own, beside, w_factor, h_row):
        return flipped(own, "cell", across), flipped(beside, "cell", across | 1), finish(w_factor, h_row)

    wanted = (need << odd) + (need_beside << (1 - odd))
    *last, w_factor = lax.switch(wanted, [late_none, late_one(0), late_one(1), late_both], own_0, lent, w_factor, h_row)
    children = place(
        labels_in, [got[-1], *last], children, [cuts[-2], always, always + rest // 2], parts
    )
    return (w_factor, h_factor, children)


SHARES = (0, 4, 13, 16)


def solution(mesh):
    placed = (P("gene", "cell"), P("cell", None), P(None, "gene"), P(None, "cell"))
    return jax.shard_map(
        steps,
        mesh=mesh,
        in_specs=placed,
        out_specs=(P(None, "gene"), P(None, "cell"), P("gene", "cell")),
        check_vma=False,
    )
```

```python
import functools

import jax
import jax.numpy as jnp
from jax import lax
from jax.experimental import pallas as pl
from jax.experimental.pallas import tpu as pltpu
from jax.sharding import PartitionSpec as P

ITERS = 2
BLOCK = 128

FLOOR = 0.0001
GRAM_EPS = 1e-06


def flipped(x, axis, mask):
    count = lax.axis_size(axis)
    return lax.ppermute(x, axis, [(i, i ^ mask) for i in range(count)])


def all_sum(x, axis, bit):
    while bit > 1:
        high, low = bit >> 1, bit >> 2
        if low:
            x = (x + flipped(x, axis, low)) + (flipped(x, axis, high) + flipped(x, axis, high | low))
        else:
            x = x + flipped(x, axis, high)
        bit = low
    return x


def row_sum(x, axis):
    odd = lax.axis_index(axis) & 1
    mine = jnp.where(odd > 0, x[1:], x[:1]) + flipped(jnp.where(odd > 0, x[:1], x[1:]), axis, 1)
    count, bit = lax.axis_size(axis), 2
    while bit < count:
        both = bit << 1 < count
        if both:
            high = bit << 1
            mine = (mine + flipped(mine, axis, bit)) + (flipped(mine, axis, high) + flipped(mine, axis, high | bit))
        else:
            mine = mine + flipped(mine, axis, bit)
        bit = bit << (2 if both else 1)
    return mine


def join_rows(mine, axis):
    odd = lax.axis_index(axis) & 1
    other = flipped(mine, axis, 1)
    return jnp.concatenate([jnp.where(odd > 0, other, mine), jnp.where(odd > 0, mine, other)])


def update_rows(factor, numer, gram):
    first = jnp.maximum(
        factor[0]
        + (numer[0] - gram[0, 0] * factor[0] - gram[0, 1] * factor[1]) / (gram[0, 0] + GRAM_EPS),
        FLOOR,
    )
    second = jnp.maximum(
        factor[1]
        + (numer[1] - gram[1, 0] * first - gram[1, 1] * factor[1]) / (gram[1, 1] + GRAM_EPS),
        FLOOR,
    )
    return jnp.stack([first, second])


def runs(first, count, parts):
    found, at = [], first
    while at < first + count:
        size = min(parts - at % parts, first + count - at)
        found.append((at // parts, at % parts, size, at - first))
        at += size
    return found


def nth(leaves, turn):
    found, low, high = 0, 0, sum(leaves)
    for b, leave in enumerate(leaves):
        found = found + jnp.where(jnp.where(leave > 0, low, high) == turn, b, 0)
        low, high = low + leave, high + 1 - leave
    return found


def my_half():
    return (lax.axis_index("cell") >= lax.axis_size("cell") // 2).astype(jnp.int32)


def lanes(block):
    return pl.ds(pl.multiple_of(block * BLOCK, BLOCK), BLOCK)


def pack_kernel(first, parts, labels, data, out, sems):
    tile = data.shape[0] // parts
    half = my_half()
    leaves = [(labels[b] != half).astype(jnp.int32) for b in range(data.shape[1] // BLOCK)]
    copies = []
    for n, (block, at, size, before) in enumerate(runs(first, out.shape[0] // tile, parts)):
        copies.append(
            pltpu.make_async_copy(
                data.at[pl.ds(at * tile, size * tile), lanes(nth(leaves, block))],
                out.at[pl.ds(before * tile, size * tile), :],
                sems.at[n],
            )
        )
        copies[-1].start()
    for copy in copies:
        copy.wait()


def pack(labels, data, first, count, parts):
    shape = (count * data.shape[0] // parts, BLOCK)
    return pl.pallas_call(
        functools.partial(pack_kernel, first, parts),
        in_specs=[pl.BlockSpec(memory_space=pltpu.SMEM), pl.BlockSpec(memory_space=pl.ANY)],
        out_specs=pl.BlockSpec(memory_space=pltpu.VMEM),
        out_shape=pltpu.VMEM(shape, data.dtype),
        scratch_shapes=[pltpu.SemaphoreType.DMA((len(runs(first, count, parts)),))],
        cost_estimate=pl.CostEstimate(flops=0, bytes_accessed=4 * shape[0] * BLOCK, transcendentals=0),
    )(labels, data)


def keep_kernel(blocks, labels, data, out):
    half = my_half()
    for b in range(blocks):
        cols = slice(b * BLOCK, (b + 1) * BLOCK)
        out[:, cols] = jnp.where(labels[b] == half, data[:, cols], jnp.zeros_like(data[:, cols]))
    out[:, blocks * BLOCK :] = jnp.zeros((out.shape[0], blocks * BLOCK), out.dtype)


def keep(labels, data):
    rows, cols = data.shape
    tile = next(t for t in (624, 312, 208, 16, rows) if rows % t == 0)
    return pl.pallas_call(
        functools.partial(keep_kernel, cols // BLOCK),
        grid=(rows // tile,),
        in_specs=[pl.BlockSpec(memory_space=pltpu.SMEM), pl.BlockSpec((tile, cols), lambda i: (i, 0))],
        out_specs=pl.BlockSpec((tile, 2 * cols), lambda i: (i, 0)),
        out_shape=jax.ShapeDtypeStruct((rows, 2 * cols), data.dtype),
        cost_estimate=pl.CostEstimate(flops=0, bytes_accessed=6 * rows * cols, transcendentals=0),
        name="keep",
    )(labels, data)


def place_kernel(pieces, parts, labels, *refs):
    got, out, sems = refs[: len(pieces)], refs[-2], refs[-1]
    tile = out.shape[0] // parts
    blocks = out.shape[1] // BLOCK // 2
    half = my_half()
    leaves = [(labels[b] == half).astype(jnp.int32) for b in range(blocks)]
    copies = []
    for ref, first in zip(got, pieces):
        for block, at, size, before in runs(first, ref.shape[0] // tile, parts):
            copy = pltpu.make_async_copy(
                ref.at[pl.ds(before * tile, size * tile), :],
                out.at[pl.ds(at * tile, size * tile), lanes(blocks + nth(leaves, block))],
                sems.at[len(copies)],
            )
            copies.append((block < sum(leaves), copy))
    for valid, copy in copies:
        pl.when(valid)(copy.start)
    for valid, copy in copies:
        pl.when(valid)(copy.wait)


def place(labels, got, held, pieces, parts):
    tile = held.shape[0] // parts
    count = sum(len(runs(first, x.shape[0] // tile, parts)) for x, first in zip(got, pieces))
    moved = sum(x.size for x in got)
    return pl.pallas_call(
        functools.partial(place_kernel, pieces, parts),
        in_specs=[pl.BlockSpec(memory_space=pltpu.SMEM)]
        + [pl.BlockSpec(memory_space=pltpu.VMEM)] * len(got)
        + [pl.BlockSpec(memory_space=pl.ANY)],
        out_specs=pl.BlockSpec(memory_space=pl.ANY),
        out_shape=jax.ShapeDtypeStruct(held.shape, held.dtype),
        input_output_aliases={len(got) + 1: 0},
        scratch_shapes=[pltpu.SemaphoreType.DMA((count,))],
        cost_estimate=pl.CostEstimate(flops=0, bytes_accessed=4 * moved, transcendentals=0),
    )(labels, *got, held)


def with_gram(part, factor):
    gram = jnp.dot(factor, factor.T, preferred_element_type=jnp.float32)
    return jnp.concatenate([part, jnp.pad(gram, ((0, 0), (0, BLOCK - factor.shape[0])))], axis=1)


def steps(data, labels, w_init, h_init):
    rows, cols = data.shape
    blocks = cols // BLOCK
    groups = lax.axis_size("cell")
    across = groups // 2
    odd = lax.axis_index("cell") & 1
    most = blocks - max(1, blocks // 4)
    parts = next(p for p in (39, 8, 4, 2) if rows % (16 * p) == 0)
    labels = labels[:, 0]
    always = max(1, most - 1) * parts
    rest = most * parts - always
    cuts = [always * share // 78 for share in SHARES]
    packed = []
    for i in range(len(cuts) - 1):
        packed.append(pack(labels, data, cuts[i], cuts[i + 1] - cuts[i], parts))
    own_0 = pack(labels, data, always, rest // 2, parts)
    own_1 = pack(labels, data, always + rest // 2, rest - rest // 2, parts)

    def send(i):
        return flipped(packed[i], "cell", across)

    got = [send(0)]
    lent = flipped(own_1, "cell", 1)
    labels_in = flipped(labels, "cell", across)
    half = my_half()
    leaving = jnp.maximum(jnp.sum((labels != half).astype(jnp.int32)), jnp.sum((labels_in == half).astype(jnp.int32)))
    need = (leaving * parts > always).astype(jnp.int32)
    need_beside = flipped(need[None], "cell", 1)[0]
    w_factor = w_init
    h_factor = h_init
    children = keep(labels, data)
    for step in range(ITERS):
        w_round = w_factor.astype(jnp.bfloat16)
        w_part = jnp.dot(w_round, data, preferred_element_type=jnp.float32)
        w_sum = all_sum(with_gram(w_part, w_round), "gene", lax.axis_size("gene"))
        h_factor = update_rows(h_factor, w_sum[:, :cols], w_sum[:, cols : cols + 2])
        h_round = h_factor.astype(jnp.bfloat16)
        h_part = lax.dot_general(
            h_round, data, (((1,), (1,)), ((), ())), preferred_element_type=jnp.float32
        )
        h_row = row_sum(with_gram(h_part, h_round), "cell")
        got.append(send(step + 1))

        def finish(w_factor, h_row):
            h_sum = join_rows(h_row, "cell")
            return update_rows(w_factor, h_sum[:, :rows], h_sum[:, rows : rows + 2])

        if step + 1 < ITERS:
            w_factor = finish(w_factor, h_row)
    children = place(labels_in, got[:-1], children, cuts[:-2], parts)

    def late_none(own, beside, w_factor, h_row):
        return jnp.zeros_like(own), jnp.zeros_like(beside), finish(w_factor, h_row)

    def late_one(parity):
        def exchange(own, beside, w_factor, h_row):
            return (
                lax.ppermute(own, "cell", [(i, i ^ across) for i in range(groups) if i % 2 == parity]),
                lax.ppermute(beside, "cell", [(i ^ 1, i ^ across) for i in range(groups) if i % 2 == parity]),
                finish(w_factor, h_row),
            )

        return exchange

    def late_both(own, beside, w_factor, h_row):
        return flipped(own, "cell", across), flipped(beside, "cell", across | 1), finish(w_factor, h_row)

    wanted = (need << odd) + (need_beside << (1 - odd))
    *last, w_factor = lax.switch(wanted, [late_none, late_one(0), late_one(1), late_both], own_0, lent, w_factor, h_row)
    children = place(
        labels_in, [got[-1], *last], children, [cuts[-2], always, always + rest // 2], parts
    )
    return (w_factor, h_factor, children)


SHARES = (0, 21, 59, 78)


def solution(mesh):
    placed = (P("gene", "cell"), P("cell", None), P(None, "gene"), P(None, "cell"))
    return jax.shard_map(
        steps,
        mesh=mesh,
        in_specs=placed,
        out_specs=(P(None, "gene"), P(None, "cell"), P("gene", "cell")),
        check_vma=False,
    )
```
